32 devices in a mesh: tm: 8 (over y, x, core), space: 4 (over z).
Axes of the slice: x: 2, y: 2, z: 4, core: 2. Of those that a mesh axis runs over, the one named last changes fastest.
Arguments:
- queries: bfloat16 [16384, 1536], P(('tm', 'space')), may hold values from -6 to 6
- key_rows: bfloat16 [16384, 1536], P(('tm', 'space')), may hold values from -6 to 6
- value_rows: bfloat16 [16384, 1536], P(('tm', 'space')), may hold values from -6 to 6
- block_list: int32 [128, 8], P(('tm', 'space')), may hold values from 0 to 127, as said below
- block_count: int32 [128], P(('tm', 'space')), may hold values from 1 to 8
Outputs:
- attended: bfloat16 [16384, 1536], P(('tm', 'space'))
The draws below stay inside these ranges and needn't reach their ends.
Inputs may be any that keep to these rules, and one draw needn't show every extreme that they name: `block_list`: the candidates of query tile t, which lies in frame f = t // 16 at block p = t % 16 of the frame and in slab s = p // 4, are: the blocks of frame f with in-frame index from s * 4 - 1 to (s + 1) * 4 that lie within the frame; and, for each b from 0 to 2 and each of the frames f - 2**b and f + 2**b that lie within the clip, its blocks with in-frame index s * 4 + j where j runs over 0 to 3 with j % 2 == b % 2. Every entry of row t, padded ones included, is such a candidate, the entries of a row are distinct, and the first entry is block t itself.
All inputs are finite; a program needn't handle non-finite values.
Results may differ from the reference program's by a relative error of at most 0.0044.
Values may be sent and summed in bfloat16 or wider, within the bound.
A program may use at most 128 MiB of HBM per device.

```python
import jax
import jax.numpy as jnp
from jax import lax

HEADS = 12
HEAD = 128
D = 1536
BLOCK = 128
BLOCKS_DEV = 4
TM_BITS = 3
LIST = 8
FRAME_BLOCKS = 16
QTILES = 128
TOKENS = 16384
N_TM = 8
N_SPACE = 4


def pair_fields(key):
    key_base = jax.random.fold_in(key, 11)
    key_one, key_two = jax.random.split(key_base, 2)
    query_field = jnp.clip(jax.random.normal(key_one, (TOKENS, D), jnp.float32), -6.0, 6.0)
    key_field = jnp.clip(jax.random.normal(key_two, (TOKENS, D), jnp.float32), -6.0, 6.0)
    return (query_field, key_field)


def draw_queries(key, part):
    return pair_fields(key)[0].astype(jnp.bfloat16)


def draw_key_rows(key, part):
    return pair_fields(key)[1].astype(jnp.bfloat16)


def mask_lists(key):
    key_base = jax.random.fold_in(key, 7)
    key_one, key_two = jax.random.split(key_base, 2)
    tile_ids = jnp.arange(QTILES, dtype=jnp.int32)
    frame_ids = tile_ids // FRAME_BLOCKS
    inner_ids = tile_ids % FRAME_BLOCKS
    slab_ids = inner_ids // BLOCKS_DEV
    local_ids = inner_ids % BLOCKS_DEV
    first_block = frame_ids * FRAME_BLOCKS + slab_ids * BLOCKS_DEV
    offsets = jnp.arange(BLOCKS_DEV + 2, dtype=jnp.int32) - 1
    near_ids = first_block[:, None] + offsets[None, :]
    near_ok = ((slab_ids[:, None] > 0) | (offsets[None, :] >= 0)) & ((slab_ids[:, None] < N_SPACE - 1) | (offsets[None, :] < BLOCKS_DEV))
    own_mark = offsets[None, :] == local_ids[:, None]
    id_parts = [near_ids]
    ok_parts = [near_ok]
    own_parts = [own_mark]
    picks_base = 2 * jnp.arange(BLOCKS_DEV // 2, dtype=jnp.int32)
    for bit_index in range(TM_BITS):
        for direction in (-1, 1):
            partner_frame = frame_ids + direction * (1 << bit_index)
            frame_ok = (partner_frame >= 0) & (partner_frame < N_TM)
            safe_frame = jnp.clip(partner_frame, 0, N_TM - 1)
            band_ids = safe_frame[:, None] * FRAME_BLOCKS + slab_ids[:, None] * BLOCKS_DEV + picks_base[None, :] + bit_index % 2
            id_parts.append(band_ids)
            ok_parts.append(jnp.broadcast_to(frame_ok[:, None], band_ids.shape))
            own_parts.append(jnp.zeros(band_ids.shape, dtype=bool))
    cand_ids = jnp.concatenate(id_parts, axis=1)
    cand_ok = jnp.concatenate(ok_parts, axis=1)
    cand_own = jnp.concatenate(own_parts, axis=1)
    width_cand = cand_ids.shape[1]
    ranks = jax.random.randint(key_one, (QTILES, width_cand), 0, 1 << 20) * width_cand + jnp.arange(width_cand, dtype=jnp.int32)[None, :]
    ranks = jnp.where(cand_own, -1, jnp.where(cand_ok, ranks, 1 << 30))
    picked = jnp.argsort(ranks, axis=1, stable=True)[:, :LIST]
    lists = jnp.take_along_axis(cand_ids, picked, axis=1).astype(jnp.int32)
    counts = jax.random.randint(key_two, (QTILES,), 1, LIST + 1)
    counts = jnp.where(tile_ids % 5 == 1, 1, counts)
    counts = jnp.where(tile_ids % 3 == 0, LIST, counts).astype(jnp.int32)
    return (lists, counts)


def draw_block_list(key, part):
    return mask_lists(key)[0]


def draw_block_count(key, part):
    return mask_lists(key)[1]


def shard_levels(rng, shape, cuts, low, largest):
    factor_of, own = 1.0, jax.random.fold_in(rng, 6)
    for dim, blocks in cuts:
        heights = jnp.exp(jax.random.uniform(jax.random.fold_in(own, dim), (blocks,), jnp.float32, low / len(cuts), largest / len(cuts)))
        factor_of = factor_of * jnp.repeat(heights, shape[dim] // blocks).reshape([-1 if axis == dim else 1 for axis in range(len(shape))])
    return factor_of


def scatter_about(rng, shape, width, bound, cuts=(), kind=jnp.bfloat16):
    loudness = shard_levels(rng, shape, cuts, -0.22, 0.18) if cuts else 1.0
    values = jax.random.normal(rng, shape, jnp.float32) * width * loudness
    return jnp.minimum(jnp.maximum(values, -bound), bound).astype(kind)


def setup_inputs(seed: int = 0) -> dict:
    key_of = jax.random.split(jax.random.key(seed), 6)
    queries = draw_queries(jax.random.fold_in(key_of[5], 71), 0)
    key_rows = draw_key_rows(jax.random.fold_in(key_of[5], 71), 0)
    value_rows = scatter_about(key_of[2], (TOKENS, D), 1.0, 6.0, ((0, 32),))
    block_list = draw_block_list(jax.random.fold_in(key_of[5], 71), 0)
    block_count = draw_block_count(jax.random.fold_in(key_of[5], 71), 0)
    return dict(queries=queries, key_rows=key_rows, value_rows=value_rows, block_list=block_list, block_count=block_count)


def reference(queries, key_rows, value_rows, block_list, block_count):
    inv_root = 1.0 / (HEAD ** 0.5)
    query_tiles = queries.reshape(QTILES, BLOCK, HEADS, HEAD)
    key_blocks = key_rows.reshape(QTILES, BLOCK, HEADS, HEAD)
    value_blocks = value_rows.reshape(QTILES, BLOCK, HEADS, HEAD)

    def tile_attend(packed):
        query_tile, picked, live_count = packed
        key_sel = key_blocks[picked].reshape(LIST * BLOCK, HEADS, HEAD)
        value_sel = value_blocks[picked].reshape(LIST * BLOCK, HEADS, HEAD)
        scores = jnp.einsum("qhd,khd->hqk", query_tile.astype(jnp.float32), key_sel.astype(jnp.float32)) * inv_root
        live_keys = (jnp.arange(LIST * BLOCK, dtype=jnp.int32) // BLOCK) < live_count
        scores = jnp.where(live_keys[None, None, :], scores, -1e30)
        row_max = jnp.max(scores, axis=-1, keepdims=True)
        weights = jnp.where(live_keys[None, None, :], jnp.exp(scores - row_max), 0.0)
        row_sum = jnp.sum(weights, axis=-1)
        rounded = lax.optimization_barrier(weights.astype(jnp.bfloat16))
        mixed_out = jnp.einsum("hqk,khd->qhd", rounded.astype(jnp.float32), value_sel.astype(jnp.float32))
        return (mixed_out / jnp.transpose(row_sum)[:, :, None]).astype(jnp.bfloat16)

    result = lax.map(tile_attend, (query_tiles, block_list, block_count))
    return result.reshape(TOKENS, D)
```

```python
import functools
import math

import jax
import jax.numpy as jnp
from jax import lax
from jax.experimental import pallas as pl
from jax.experimental.pallas import tpu as pltpu
from jax.sharding import PartitionSpec as P

HEAD = 128
BLOCK = 128
DEAD = -1e30
MESH = pl.DeviceIdType.MESH


def kernel(
    tm_count, space_count, list_width,
    q_hbm, k_hbm, v_hbm, list_ref, count_ref, o_ref,
    q_own, k_own, v_own, k_halo, v_halo, k_band, v_band,
    top, total, mixed, near_bias, band_bias,
    local_sem, halo_send, halo_recv, band_send, band_recv, relay_send,
):
    rows, width = q_hbm.shape
    blocks = rows // BLOCK
    picks = blocks // 2
    heads = width // HEAD
    bits = tm_count.bit_length() - 1
    half = tm_count // 2
    relayed = bits == 3
    frame = lax.axis_index("tm")
    slab = lax.axis_index("space")
    scale = math.log2(math.e) / HEAD**0.5

    def flag(pred):
        return jnp.where(pred, 1, 0)

    def exists(delta):
        return (frame + delta >= 0) & (frame + delta < tm_count)

    def slab_exists(delta):
        return (slab + delta >= 0) & (slab + delta < space_count)

    barrier = pltpu.get_barrier_semaphore()
    greets = []
    for delta in (-1, 1):
        greets.append((slab_exists(delta), {"space": slab + delta}))
    for bit in range(bits):
        for delta in (-(1 << bit), 1 << bit):
            greets.append((exists(delta), {"tm": frame + delta}))
    if relayed:
        greets.append((frame == 0, {"tm": frame + half - 1}))
        greets.append((frame == half - 1, {"tm": frame - half + 1}))
        greets.append((frame == tm_count - 1, {"tm": frame - half + 1}))
        greets.append((frame == half, {"tm": frame + half - 1}))
    expected = 0
    for pred, device in greets:
        expected = expected + flag(pred)

        @pl.when(pred)
        def _(device=device):
            pl.semaphore_signal(barrier, inc=1, device_id=device, device_id_type=MESH)

    pl.semaphore_wait(barrier, expected)

    def halo_copies(side, delta):
        start = (blocks - 1) * BLOCK if side == 0 else 0
        for index, (src, dst) in enumerate(((k_hbm, k_halo), (v_hbm, v_halo))):
            yield pltpu.make_async_remote_copy(
                src_ref=src.at[pl.ds(start, BLOCK)],
                dst_ref=dst.at[side],
                send_sem=halo_send.at[side, index],
                recv_sem=halo_recv.at[side, index],
                device_id={"space": slab + delta},
                device_id_type=MESH,
            )

    def band_copy(bit, side, chunk, device):
        pick, which = chunk // 2, chunk % 2
        src = (k_hbm, v_hbm)[which]
        dst = (k_band, v_band)[which]
        slot = 2 * bit + side
        return pltpu.make_async_remote_copy(
            src_ref=src.at[pl.ds((2 * pick + bit % 2) * BLOCK, BLOCK)],
            dst_ref=dst.at[slot, pl.ds(pick * BLOCK, BLOCK)],
            send_sem=band_send.at[slot, chunk],
            recv_sem=band_recv.at[slot, chunk],
            device_id={"tm": device},
            device_id_type=MESH,
        )

    def relay_copy(kind, slot_from, slot_to, chunk, device):
        pick, which = chunk // 2, chunk % 2
        buf = (k_band, v_band)[which]
        return pltpu.make_async_remote_copy(
            src_ref=buf.at[slot_from, pl.ds(pick * BLOCK, BLOCK)],
            dst_ref=buf.at[slot_to, pl.ds(pick * BLOCK, BLOCK)],
            send_sem=relay_send.at[kind, chunk],
            recv_sem=band_recv.at[slot_to, chunk],
            device_id={"tm": device},
            device_id_type=MESH,
        )

    def sends(bit, side):
        delta = (1 << bit) if side == 0 else -(1 << bit)
        pred = exists(delta)
        if relayed and bit == 0:
            pred = pred & (frame != (half - 1 if side == 0 else half))
        if relayed and bit == 1:
            if side == 0:
                pred = pred & ((frame < half - 2) | (frame >= half))
            else:
                pred = pred & ((frame < half) | (frame >= half + 2))
        return pred, frame + delta

    chunks = 2 * picks
    for side, delta in ((0, 1), (1, -1)):

        @pl.when(slab_exists(delta))
        def _(side=side, delta=delta):
            for copy in halo_copies(side, delta):
                copy.start()

    order = list(range(1, bits)) + [0]
    for chunk in range(chunks):
        for bit in order:
            for side in (0, 1):
                pred, device = sends(bit, side)

                @pl.when(pred)
                def _(bit=bit, side=side, chunk=chunk, device=device):
                    band_copy(bit, side, chunk, device).start()

    local = [
        pltpu.make_async_copy(src, dst, local_sem.at[index])
        for index, (src, dst) in enumerate(((q_hbm, q_own), (k_hbm, k_own), (v_hbm, v_own)))
    ]
    for copy in local:
        copy.start()

    frame_blocks = blocks * space_count
    first_block = frame * frame_blocks + slab * blocks

    def bias_rows(ids):
        row = jnp.concatenate([jnp.full((1, BLOCK), ident, jnp.int32) for ident in ids], axis=1)
        out = []
        for tile in range(blocks):
            count = count_ref[tile]
            value = jnp.full(row.shape, DEAD, jnp.float32)
            for entry in range(list_width):
                listed = jnp.where(entry < count, list_ref[tile, entry], -1)
                value = jnp.where(row == listed, 0.0, value)
            out.append(value)
        return out

    near_ids = [first_block + c for c in range(blocks)] + [first_block - 1, first_block + blocks]
    for tile, value in enumerate(bias_rows(near_ids)):
        near_bias[tile : tile + 1, :] = value
    for bit in range(bits):
        for side in (0, 1):
            partner = frame - (1 << bit) if side == 0 else frame + (1 << bit)
            ids = [
                partner * frame_blocks + slab * blocks + 2 * pick + bit % 2
                for pick in range(picks)
            ]
            for tile, value in enumerate(bias_rows(ids)):
                band_bias[2 * bit + side, tile : tile + 1, :] = value

    for copy in local:
        copy.wait()

    def attend(get_k, get_v, get_bias, keys, first):
        ones = jnp.ones((keys, HEAD), jnp.bfloat16)

        def one_head(head, carry):
            cols = pl.ds(pl.multiple_of(head * HEAD, HEAD), HEAD)
            raw = lax.dot_general(
                q_own[:, cols], get_k(cols), (((1,), (1,)), ((), ())),
                preferred_element_type=jnp.float32,
            )
            parts, shrink = [], []
            for tile in range(blocks):
                span = slice(tile * BLOCK, (tile + 1) * BLOCK)
                scores = raw[span] * scale + get_bias(tile)
                peak = jnp.max(scores, axis=1, keepdims=True)
                if first:
                    new_top = jnp.broadcast_to(peak, (BLOCK, HEAD))
                else:
                    old_top = top[head, span, :]
                    new_top = jnp.maximum(old_top, peak)
                    shrink.append(jnp.exp2(old_top - new_top))
                top[head, span, :] = new_top
                wide = jnp.concatenate([new_top] * (keys // HEAD), axis=1)
                parts.append(jnp.exp2(scores - wide).astype(jnp.bfloat16))
            weights = jnp.concatenate(parts, axis=0)
            extended = jnp.concatenate([get_v(cols), ones], axis=1)
            both = jnp.dot(weights, extended, preferred_element_type=jnp.float32)
            if first:
                mixed[head] = both[:, :HEAD]
                total[head] = both[:, HEAD:]
            else:
                factor = jnp.concatenate(shrink, axis=0)
                mixed[head] = mixed[head] * factor + both[:, :HEAD]
                total[head] = total[head] * factor + both[:, HEAD:]
            return carry

        lax.fori_loop(0, heads, one_head, 0)

    attend(
        lambda cols: k_own[:, cols],
        lambda cols: v_own[:, cols],
        lambda tile: near_bias[tile : tile + 1, : blocks * BLOCK],
        blocks * BLOCK,
        True,
    )

    def halo(side, delta):
        @pl.when(slab_exists(delta))
        def _():
            for copy in halo_copies(side, delta):
                copy.wait_recv()
            start = (blocks + side) * BLOCK
            attend(
                lambda cols: k_halo[side, :, cols],
                lambda cols: v_halo[side, :, cols],
                lambda tile: near_bias[tile : tile + 1, start : start + BLOCK],
                BLOCK,
                False,
            )

    halo(0, -1)
    halo(1, 1)

    def band_wait(bit, side, chunk):
        slot = 2 * bit + side
        pick, which = chunk // 2, chunk % 2
        buf = (k_band, v_band)[which]
        pltpu.make_async_remote_copy(
            src_ref=(k_hbm, v_hbm)[which].at[pl.ds(0, BLOCK)],
            dst_ref=buf.at[slot, pl.ds(pick * BLOCK, BLOCK)],
            send_sem=band_send.at[slot, chunk],
            recv_sem=band_recv.at[slot, chunk],
            device_id={"tm": frame},
            device_id_type=MESH,
        ).wait_recv()

    early = frame < half
    outer = (frame < 2) | (frame >= tm_count - 2)
    corner = (frame == 0) | (frame == tm_count - 1)
    inward = flag(early)
    last = bits - 1
    relay_pair = (
        (outer, lambda chunk: relay_copy(
            0, 2 + inward, 3 - inward, chunk, jnp.where(early, frame + half, frame - half))),
        (corner, lambda chunk: relay_copy(
            1, 2 * last + inward, inward, chunk, jnp.where(early, half - 1, half))),
    )
    if relayed:
        for chunk in range(chunks):
            for (pred, make), bit in zip(relay_pair, (1, last)):

                @pl.when(pred)
                def _(make=make, bit=bit, chunk=chunk):
                    band_wait(bit, inward, chunk)
                    make(chunk).start()

    def band(bit, side, waited):
        delta = jnp.where(side == 0, -(1 << bit), 1 << bit)

        @pl.when(exists(delta))
        def _():
            @pl.when(jnp.logical_not(waited))
            def _():
                for chunk in range(chunks):
                    band_wait(bit, side, chunk)

            slot = 2 * bit + side
            attend(
                lambda cols: k_band[slot, :, cols],
                lambda cols: v_band[slot, :, cols],
                lambda tile: band_bias[slot, tile : tile + 1, :],
                picks * BLOCK,
                False,
            )

    never = frame < 0
    other = 1 - inward
    core_side = 1 - lax.rem(frame, 2)
    relay_b = outer if relayed else never
    relay_a = corner if relayed else never
    band(0, core_side, never)
    for bit in range(2, bits - 1):
        band(bit, other, never)
        band(bit, inward, never)
    band(last, inward, relay_a)
    if bits > 1:
        band(1, other, never)
    band(0, 1 - core_side, never)
    if bits > 1:
        band(1, inward, relay_b)

    def finish(head, carry):
        cols = pl.ds(pl.multiple_of(head * HEAD, HEAD), HEAD)
        o_ref[:, cols] = (mixed[head] / total[head]).astype(o_ref.dtype)
        return carry

    lax.fori_loop(0, heads, finish, 0)

    for side, delta in ((0, 1), (1, -1)):

        @pl.when(slab_exists(delta))
        def _(side=side, delta=delta):
            for copy in halo_copies(side, delta):
                copy.wait_send()

    for bit in range(bits):
        for side in (0, 1):
            pred, device = sends(bit, side)

            @pl.when(pred)
            def _(bit=bit, side=side, device=device):
                for chunk in range(chunks):
                    band_copy(bit, side, chunk, device).wait_send()

    if relayed:
        for pred, make in relay_pair:

            @pl.when(pred)
            def _(make=make):
                for chunk in range(chunks):
                    make(chunk).wait_send()


def shards(tm_count, space_count, queries, key_rows, value_rows, block_list, block_count):
    rows, width = queries.shape
    blocks = rows // BLOCK
    picks = blocks // 2
    heads = width // HEAD
    slots = 2 * (tm_count.bit_length() - 1)
    kind = key_rows.dtype
    anywhere = pl.BlockSpec(memory_space=pl.ANY)
    scalar = pl.BlockSpec(memory_space=pltpu.SMEM)
    dma = pltpu.SemaphoreType.DMA
    return pl.pallas_call(
        functools.partial(kernel, tm_count, space_count, block_list.shape[1]),
        out_shape=jax.ShapeDtypeStruct((rows, width), queries.dtype),
        in_specs=[anywhere, anywhere, anywhere, scalar, scalar],
        out_specs=pl.BlockSpec(memory_space=pltpu.VMEM),
        scratch_shapes=[
            pltpu.VMEM((rows, width), kind),
            pltpu.VMEM((rows, width), kind),
            pltpu.VMEM((rows, width), kind),
            pltpu.VMEM((2, BLOCK, width), kind),
            pltpu.VMEM((2, BLOCK, width), kind),
            pltpu.VMEM((slots, picks * BLOCK, width), kind),
            pltpu.VMEM((slots, picks * BLOCK, width), kind),
            pltpu.VMEM((heads, rows, HEAD), jnp.float32),
            pltpu.VMEM((heads, rows, HEAD), jnp.float32),
            pltpu.VMEM((heads, rows, HEAD), jnp.float32),
            pltpu.VMEM((blocks, (blocks + 2) * BLOCK), jnp.float32),
            pltpu.VMEM((slots, blocks, picks * BLOCK), jnp.float32),
            dma((3,)),
            dma((2, 2)),
            dma((2, 2)),
            dma((slots, 2 * picks)),
            dma((slots, 2 * picks)),
            dma((2, 2 * picks)),
        ],
        compiler_params=pltpu.CompilerParams(
            collective_id=0, has_side_effects=True, vmem_limit_bytes=60 * 1024 * 1024
        ),
    )(queries, key_rows, value_rows, block_list, block_count)


def solution(mesh):
    placed = (
        P(("tm", "space"), None),
        P(("tm", "space"), None),
        P(("tm", "space"), None),
        P(("tm", "space"), None),
        P(("tm", "space")),
    )
    return jax.shard_map(
        functools.partial(shards, mesh.shape["tm"], mesh.shape["space"]),
        mesh=mesh, in_specs=placed, out_specs=P(("tm", "space"), None), check_vma=False,
    )
```

```python
import functools
import math

import jax
import jax.numpy as jnp
from jax import lax
from jax.experimental import pallas as pl
from jax.experimental.pallas import tpu as pltpu
from jax.sharding import PartitionSpec as P

HEAD = 128
BLOCK = 128
DEAD = -1e30
MESH = pl.DeviceIdType.MESH


def kernel(
    tm_count, space_count, list_width, parts,
    q_hbm, k_hbm, v_hbm, list_ref, count_ref, o_ref,
    q_own, k_own, v_own, k_halo, v_halo, k_band, v_band,
    top, total, mixed, near_bias, band_bias,
    local_sem, halo_send, halo_recv, band_send, band_recv, relay_send,
):
    rows, width = q_hbm.shape
    blocks = rows // BLOCK
    picks = blocks // 2
    heads = width // HEAD
    bits = tm_count.bit_length() - 1
    half = tm_count // 2
    relayed = bits == 3
    frame = lax.axis_index("tm")
    slab = lax.axis_index("space")
    scale = math.log2(math.e) / HEAD**0.5

    def flag(pred):
        return jnp.where(pred, 1, 0)

    def exists(delta):
        return (frame + delta >= 0) & (frame + delta < tm_count)

    def slab_exists(delta):
        return (slab + delta >= 0) & (slab + delta < space_count)

    barrier = pltpu.get_barrier_semaphore()
    greets = []
    for delta in (-1, 1):
        greets.append((slab_exists(delta), {"space": slab + delta}))
    for bit in range(bits):
        for delta in (-(1 << bit), 1 << bit):
            greets.append((exists(delta), {"tm": frame + delta}))
    if relayed:
        greets.append((frame == 0, {"tm": frame + half - 1}))
        greets.append((frame == half - 1, {"tm": frame - half + 1}))
        greets.append((frame == tm_count - 1, {"tm": frame - half + 1}))
        greets.append((frame == half, {"tm": frame + half - 1}))
    expected = 0
    for pred, device in greets:
        expected = expected + flag(pred)

        @pl.when(pred)
        def _(device=device):
            pl.semaphore_signal(barrier, inc=1, device_id=device, device_id_type=MESH)

    pl.semaphore_wait(barrier, expected)

    def halo_copies(side, delta):
        start = (blocks - 1) * BLOCK if side == 0 else 0
        for index, (src, dst) in enumerate(((k_hbm, k_halo), (v_hbm, v_halo))):
            yield pltpu.make_async_remote_copy(
                src_ref=src.at[pl.ds(start, BLOCK)],
                dst_ref=dst.at[side],
                send_sem=halo_send.at[side, index],
                recv_sem=halo_recv.at[side, index],
                device_id={"space": slab + delta},
                device_id_type=MESH,
            )

    part_width = width // parts

    def part_cols(part):
        return pl.ds(pl.multiple_of(part * part_width, part_width), part_width)

    def band_copies(bit, side, part, device):
        slot = 2 * bit + side
        for which, (src, dst) in enumerate(((k_hbm, k_band), (v_hbm, v_band))):
            yield pltpu.make_async_remote_copy(
                src_ref=src.reshape(picks, 2, BLOCK, width).at[:, bit % 2, :, part_cols(part)],
                dst_ref=dst.at[slot, :, :, part_cols(part)],
                send_sem=band_send.at[slot, part, which],
                recv_sem=band_recv.at[slot, part, which],
                device_id={"tm": device},
                device_id_type=MESH,
            )

    def relay_copies(kind, slot_from, slot_to, part, device):
        for which, buf in enumerate((k_band, v_band)):
            yield pltpu.make_async_remote_copy(
                src_ref=buf.at[slot_from, :, :, part_cols(part)],
                dst_ref=buf.at[slot_to, :, :, part_cols(part)],
                send_sem=relay_send.at[kind, part, which],
                recv_sem=band_recv.at[slot_to, part, which],
                device_id={"tm": device},
                device_id_type=MESH,
            )

    def sends(bit, side):
        delta = (1 << bit) if side == 0 else -(1 << bit)
        pred = exists(delta)
        if relayed and bit == 0:
            pred = pred & (frame != (half - 1 if side == 0 else half))
        if relayed and bit == 1:
            if side == 0:
                pred = pred & ((frame < half - 2) | (frame >= half))
            else:
                pred = pred & ((frame < half) | (frame >= half + 2))
        return pred, frame + delta

    for side, delta in ((0, 1), (1, -1)):

        @pl.when(slab_exists(delta))
        def _(side=side, delta=delta):
            for copy in halo_copies(side, delta):
                copy.start()

    order = list(range(1, bits)) + [0]
    for bit in order:
        for side in (0, 1):
            pred, device = sends(bit, side)

            @pl.when(pred)
            def _(bit=bit, side=side, device=device):
                for part in range(parts):
                    for copy in band_copies(bit, side, part, device):
                        copy.start()

    local = [
        pltpu.make_async_copy(src, dst, local_sem.at[index])
        for index, (src, dst) in enumerate(((q_hbm, q_own), (k_hbm, k_own), (v_hbm, v_own)))
    ]
    for copy in local:
        copy.start()

    frame_blocks = blocks * space_count
    first_block = frame * frame_blocks + slab * blocks

    def bias_rows(ids):
        row = jnp.concatenate([jnp.full((1, BLOCK), ident, jnp.int32) for ident in ids], axis=1)
        out = []
        for tile in range(blocks):
            count = count_ref[tile]
            value = jnp.full(row.shape, DEAD, jnp.float32)
            for entry in range(list_width):
                listed = jnp.where(entry < count, list_ref[tile, entry], -1)
                value = jnp.where(row == listed, 0.0, value)
            out.append(value)
        return out

    near_ids = [first_block + c for c in range(blocks)] + [first_block - 1, first_block + blocks]
    for tile, value in enumerate(bias_rows(near_ids)):
        near_bias[tile : tile + 1, :] = value
    for bit in range(bits):
        for side in (0, 1):
            partner = frame - (1 << bit) if side == 0 else frame + (1 << bit)
            ids = [
                partner * frame_blocks + slab * blocks + 2 * pick + bit % 2
                for pick in range(picks)
            ]
            for tile, value in enumerate(bias_rows(ids)):
                band_bias[2 * bit + side, tile : tile + 1, :] = value

    for copy in local:
        copy.wait()

    def attend(get_k, get_v, get_bias, keys, first=False, final=False, bounds=None):
        ones = jnp.ones((keys, HEAD), jnp.bfloat16)

        def one_head(head, carry):
            cols = pl.ds(pl.multiple_of(head * HEAD, HEAD), HEAD)
            raw = lax.dot_general(
                q_own[:, cols], get_k(cols), (((1,), (1,)), ((), ())),
                preferred_element_type=jnp.float32,
            )
            parts, shrink = [], []
            for tile in range(blocks):
                span = slice(tile * BLOCK, (tile + 1) * BLOCK)
                scores = raw[span] * scale + get_bias(tile)
                peak = jnp.max(scores, axis=1, keepdims=True)
                if first:
                    new_top = jnp.broadcast_to(peak, (BLOCK, HEAD))
                else:
                    old_top = top[head, span, :]
                    new_top = jnp.maximum(old_top, peak)
                    shrink.append(jnp.exp2(old_top - new_top))
                if not final:
                    top[head, span, :] = new_top
                wide = jnp.concatenate([new_top] * (keys // HEAD), axis=1)
                parts.append(jnp.exp2(scores - wide).astype(jnp.bfloat16))
            weights = jnp.concatenate(parts, axis=0)
            extended = jnp.concatenate([get_v(cols), ones], axis=1)
            both = jnp.dot(weights, extended, preferred_element_type=jnp.float32)
            if first:
                mixed[head] = both[:, :HEAD]
                total[head] = both[:, HEAD:]
            else:
                factor = jnp.concatenate(shrink, axis=0)
                new_mixed = mixed[head] * factor + both[:, :HEAD]
                new_total = total[head] * factor + both[:, HEAD:]
                if final:
                    o_ref[:, cols] = (new_mixed / new_total).astype(o_ref.dtype)
                else:
                    mixed[head] = new_mixed
                    total[head] = new_total
            return carry

        low, high = (0, heads) if bounds is None else bounds
        lax.fori_loop(low, high, one_head, 0)

    attend(
        lambda cols: k_own[:, cols],
        lambda cols: v_own[:, cols],
        lambda tile: near_bias[tile : tile + 1, : blocks * BLOCK],
        blocks * BLOCK,
        first=True,
    )

    def halo(side, delta):
        @pl.when(slab_exists(delta))
        def _():
            for copy in halo_copies(side, delta):
                copy.wait_recv()
            start = (blocks + side) * BLOCK
            attend(
                lambda cols: k_halo[side, :, cols],
                lambda cols: v_halo[side, :, cols],
                lambda tile: near_bias[tile : tile + 1, start : start + BLOCK],
                BLOCK,
            )

    halo(0, -1)
    halo(1, 1)

    def band_wait(bit, side, part):
        slot = 2 * bit + side
        for which, (src, dst) in enumerate(((k_hbm, k_band), (v_hbm, v_band))):
            pltpu.make_async_remote_copy(
                src_ref=src.reshape(picks, 2, BLOCK, width).at[:, 0, :, part_cols(part)],
                dst_ref=dst.at[slot, :, :, part_cols(part)],
                send_sem=band_send.at[slot, part, which],
                recv_sem=band_recv.at[slot, part, which],
                device_id={"tm": frame},
                device_id_type=MESH,
            ).wait_recv()

    early = frame < half
    outer = (frame < 2) | (frame >= tm_count - 2)
    corner = (frame == 0) | (frame == tm_count - 1)
    inward = flag(early)
    last = bits - 1
    relay_pair = (
        (outer, lambda part: relay_copies(
            0, 2 + inward, 3 - inward, part, jnp.where(early, frame + half, frame - half))),
        (corner, lambda part: relay_copies(
            1, 2 * last + inward, inward, part, jnp.where(early, half - 1, half))),
    )
    if relayed:
        for part in range(parts):
            for (pred, make), bit in zip(relay_pair, (1, last)):

                @pl.when(pred)
                def _(make=make, bit=bit, part=part):
                    band_wait(bit, inward, part)
                    for copy in make(part):
                        copy.start()

    def band_exists(bit, side):
        return exists(jnp.where(side == 0, -(1 << bit), 1 << bit))

    def band_keys(slot):
        return (
            lambda cols: k_band[slot, :, :, cols].reshape(picks * BLOCK, HEAD),
            lambda cols: v_band[slot, :, :, cols].reshape(picks * BLOCK, HEAD),
            lambda tile: band_bias[slot, tile : tile + 1, :],
        )

    def band(bit, side, waited):
        @pl.when(band_exists(bit, side))
        def _():
            @pl.when(jnp.logical_not(waited))
            def _():
                for part in range(parts):
                    band_wait(bit, side, part)

            attend(*band_keys(2 * bit + side), picks * BLOCK)

    never = frame < 0
    other = 1 - inward
    core_side = 1 - lax.rem(frame, 2)
    relay_a = corner if relayed else never
    relay_b = outer if relayed else never
    band(0, core_side, never)
    for bit in range(2, bits - 1):
        band(bit, other, never)
        band(bit, inward, never)
    band(last, inward, relay_a)
    band(1, other, never)

    late = ((0, 1 - core_side, never), (1, inward, relay_b))
    both_exist = band_exists(0, 1 - core_side) & band_exists(1, inward)
    heads_part = heads // parts

    @pl.when(both_exist)
    def _():
        getters = [band_keys(2 * bit + side) for bit, side, _ in late]

        def joined(index, axis):
            return lambda arg: jnp.concatenate([g[index](arg) for g in getters], axis=axis)

        def one_part(part, carry):
            for bit, side, waited in late:

                @pl.when(jnp.logical_not(waited))
                def _(bit=bit, side=side):
                    band_wait(bit, side, part)

            attend(
                joined(0, 0), joined(1, 0), joined(2, 1), 2 * picks * BLOCK,
                final=True, bounds=(part * heads_part, (part + 1) * heads_part),
            )
            return carry

        lax.fori_loop(0, parts, one_part, 0)

    @pl.when(jnp.logical_not(both_exist))
    def _():
        for bit, side, waited in late:
            band(bit, side, waited)

        def finish(head, carry):
            cols = pl.ds(pl.multiple_of(head * HEAD, HEAD), HEAD)
            o_ref[:, cols] = (mixed[head] / total[head]).astype(o_ref.dtype)
            return carry

        lax.fori_loop(0, heads, finish, 0)

    for side, delta in ((0, 1), (1, -1)):

        @pl.when(slab_exists(delta))
        def _(side=side, delta=delta):
            for copy in halo_copies(side, delta):
                copy.wait_send()

    for bit in range(bits):
        for side in (0, 1):
            pred, device = sends(bit, side)

            @pl.when(pred)
            def _(bit=bit, side=side, device=device):
                for part in range(parts):
                    for copy in band_copies(bit, side, part, device):
                        copy.wait_send()

    if relayed:
        for pred, make in relay_pair:

            @pl.when(pred)
            def _(make=make):
                for part in range(parts):
                    for copy in make(part):
                        copy.wait_send()


def shards(tm_count, space_count, queries, key_rows, value_rows, block_list, block_count):
    rows, width = queries.shape
    blocks = rows // BLOCK
    picks = blocks // 2
    heads = width // HEAD
    slots = 2 * (tm_count.bit_length() - 1)
    kind = key_rows.dtype
    parts = math.gcd(heads, 6)
    anywhere = pl.BlockSpec(memory_space=pl.ANY)
    scalar = pl.BlockSpec(memory_space=pltpu.SMEM)
    dma = pltpu.SemaphoreType.DMA
    return pl.pallas_call(
        functools.partial(kernel, tm_count, space_count, block_list.shape[1], parts),
        out_shape=jax.ShapeDtypeStruct((rows, width), queries.dtype),
        in_specs=[anywhere, anywhere, anywhere, scalar, scalar],
        out_specs=pl.BlockSpec(memory_space=pltpu.VMEM),
        scratch_shapes=[
            pltpu.VMEM((rows, width), kind),
            pltpu.VMEM((rows, width), kind),
            pltpu.VMEM((rows, width), kind),
            pltpu.VMEM((2, BLOCK, width), kind),
            pltpu.VMEM((2, BLOCK, width), kind),
            pltpu.VMEM((slots, picks, BLOCK, width), kind),
            pltpu.VMEM((slots, picks, BLOCK, width), kind),
            pltpu.VMEM((heads, rows, HEAD), jnp.float32),
            pltpu.VMEM((heads, rows, HEAD), jnp.float32),
            pltpu.VMEM((heads, rows, HEAD), jnp.float32),
            pltpu.VMEM((blocks, (blocks + 2) * BLOCK), jnp.float32),
            pltpu.VMEM((slots, blocks, picks * BLOCK), jnp.float32),
            dma((3,)),
            dma((2, 2)),
            dma((2, 2)),
            dma((slots, parts, 2)),
            dma((slots, parts, 2)),
            dma((2, parts, 2)),
        ],
        compiler_params=pltpu.CompilerParams(
            collective_id=0, has_side_effects=True, vmem_limit_bytes=60 * 1024 * 1024
        ),
    )(queries, key_rows, value_rows, block_list, block_count)


def solution(mesh):
    placed = (
        P(("tm", "space"), None),
        P(("tm", "space"), None),
        P(("tm", "space"), None),
        P(("tm", "space"), None),
        P(("tm", "space")),
    )
    return jax.shard_map(
        functools.partial(shards, mesh.shape["tm"], mesh.shape["space"]),
        mesh=mesh, in_specs=placed, out_specs=P(("tm", "space"), None), check_vma=False,
    )
```

```python
import functools
import math

import jax
import jax.numpy as jnp
from jax import lax
from jax.experimental import pallas as pl
from jax.experimental.pallas import tpu as pltpu
from jax.sharding import PartitionSpec as P

HEAD = 128
BLOCK = 128
DEAD = -1e30
MESH = pl.DeviceIdType.MESH


def kernel(
    tm_count, space_count, list_width, parts,
    q_hbm, k_hbm, v_hbm, list_hbm, count_hbm, o_ref,
    list_ref, count_ref,
    q_own, k_own, v_own, k_halo, v_halo, k_band, v_band,
    top, total, mixed, near_bias, band_bias,
    local_sem, halo_send, halo_recv, band_send, band_recv, relay_send,
):
    rows, width = q_hbm.shape
    blocks = rows // BLOCK
    picks = blocks // 2
    heads = width // HEAD
    bits = tm_count.bit_length() - 1
    half = tm_count // 2
    relayed = bits == 3
    frame = lax.axis_index("tm")
    slab = lax.axis_index("space")
    scale = math.log2(math.e) / HEAD**0.5

    def flag(pred):
        return jnp.where(pred, 1, 0)

    def exists(delta):
        return (frame + delta >= 0) & (frame + delta < tm_count)

    def slab_exists(delta):
        return (slab + delta >= 0) & (slab + delta < space_count)

    def sends(bit, side):
        delta = (1 << bit) if side == 0 else -(1 << bit)
        pred = exists(delta)
        if relayed and bit == 0:
            pred = pred & (frame != (half - 1 if side == 0 else half))
        if relayed and bit == 1:
            if side == 0:
                pred = pred & ((frame < half - 2) | (frame >= half))
            else:
                pred = pred & ((frame < half) | (frame >= half + 2))
        return pred, frame + delta

    barrier = pltpu.get_barrier_semaphore()
    greets = []
    for delta in (-1, 1):
        greets.append((slab_exists(delta), {"space": slab + delta}))
    for bit in range(bits):
        for side in (0, 1):
            pred, device = sends(bit, side)
            greets.append((pred, {"tm": device}))
    if relayed:
        greets.append((frame == 0, {"tm": frame + half - 1}))
        greets.append((frame == half - 1, {"tm": frame - half + 1}))
        greets.append((frame == tm_count - 1, {"tm": frame - half + 1}))
        greets.append((frame == half, {"tm": frame + half - 1}))
    expected = 0
    for pred, device in greets:
        expected = expected + flag(pred)

        @pl.when(pred)
        def _(device=device):
            pl.semaphore_signal(barrier, inc=1, device_id=device, device_id_type=MESH)

    pl.semaphore_wait(barrier, expected)

    def halo_copies(side, delta):
        start = (blocks - 1) * BLOCK if side == 0 else 0
        for index, (src, dst) in enumerate(((k_hbm, k_halo), (v_hbm, v_halo))):
            yield pltpu.make_async_remote_copy(
                src_ref=src.at[pl.ds(start, BLOCK)],
                dst_ref=dst.at[side],
                send_sem=halo_send.at[side, index],
                recv_sem=halo_recv.at[side, index],
                device_id={"space": slab + delta},
                device_id_type=MESH,
            )

    part_width = width // parts

    def part_cols(part):
        return pl.ds(pl.multiple_of(part * part_width, part_width), part_width)

    def band_copies(bit, side, part, device):
        slot = 2 * bit + side
        for which, (src, dst) in enumerate(((k_hbm, k_band), (v_hbm, v_band))):
            yield pltpu.make_async_remote_copy(
                src_ref=src.reshape(picks, 2, BLOCK, width).at[:, bit % 2, :, part_cols(part)],
                dst_ref=dst.at[slot, :, :, part_cols(part)],
                send_sem=band_send.at[slot, part, which],
                recv_sem=band_recv.at[slot, part, which],
                device_id={"tm": device},
                device_id_type=MESH,
            )

    def relay_copies(kind, slot_from, slot_to, part, device):
        for which, buf in enumerate((k_band, v_band)):
            yield pltpu.make_async_remote_copy(
                src_ref=buf.at[slot_from, :, :, part_cols(part)],
                dst_ref=buf.at[slot_to, :, :, part_cols(part)],
                send_sem=relay_send.at[kind, part, which],
                recv_sem=band_recv.at[slot_to, part, which],
                device_id={"tm": device},
                device_id_type=MESH,
            )

    for side, delta in ((0, 1), (1, -1)):

        @pl.when(slab_exists(delta))
        def _(side=side, delta=delta):
            for copy in halo_copies(side, delta):
                copy.start()

    order = list(range(1, bits)) + [0]
    for bit in order:
        for side in (0, 1):
            pred, device = sends(bit, side)

            @pl.when(pred)
            def _(bit=bit, side=side, device=device):
                for part in range(parts):
                    for copy in band_copies(bit, side, part, device):
                        copy.start()

    local = [
        pltpu.make_async_copy(src, dst, local_sem.at[index])
        for index, (src, dst) in enumerate((
            (q_hbm, q_own), (k_hbm, k_own), (v_hbm, v_own),
            (list_hbm, list_ref), (count_hbm, count_ref),
        ))
    ]
    for copy in local:
        copy.start()

    for copy in local[3:]:
        copy.wait()

    frame_blocks = blocks * space_count
    first_block = frame * frame_blocks + slab * blocks

    def bias_rows(ids):
        row = jnp.concatenate([jnp.full((1, BLOCK), ident, jnp.int32) for ident in ids], axis=1)
        out = []
        for tile in range(blocks):
            count = count_ref[tile]
            value = jnp.full(row.shape, DEAD, jnp.float32)
            for entry in range(list_width):
                listed = jnp.where(entry < count, list_ref[tile, entry], -1)
                value = jnp.where(row == listed, 0.0, value)
            out.append(value)
        return out

    near_ids = [first_block + c for c in range(blocks)] + [first_block - 1, first_block + blocks]
    for tile, value in enumerate(bias_rows(near_ids)):
        near_bias[tile : tile + 1, :] = value
    for bit in range(bits):
        for side in (0, 1):
            partner = frame - (1 << bit) if side == 0 else frame + (1 << bit)
            ids = [
                partner * frame_blocks + slab * blocks + 2 * pick + bit % 2
                for pick in range(picks)
            ]
            for tile, value in enumerate(bias_rows(ids)):
                band_bias[2 * bit + side, tile : tile + 1, :] = value

    for copy in local[:3]:
        copy.wait()

    def attend(get_k, get_v, get_bias, keys, first=False, final=False, bounds=None):
        ones = jnp.ones((keys, HEAD), jnp.bfloat16)

        def one_head(head, carry):
            cols = pl.ds(pl.multiple_of(head * HEAD, HEAD), HEAD)
            raw = lax.dot_general(
                q_own[:, cols], get_k(cols), (((1,), (1,)), ((), ())),
                preferred_element_type=jnp.float32,
            )
            parts, shrink = [], []
            for tile in range(blocks):
                span = slice(tile * BLOCK, (tile + 1) * BLOCK)
                scores = raw[span] * scale + get_bias(tile)
                peak = jnp.max(scores, axis=1, keepdims=True)
                if first:
                    new_top = jnp.broadcast_to(peak, (BLOCK, HEAD))
                else:
                    old_top = top[head, span, :]
                    new_top = jnp.maximum(old_top, peak)
                    shrink.append(jnp.exp2(old_top - new_top))
                if not final:
                    top[head, span, :] = new_top
                wide = jnp.concatenate([new_top] * (keys // HEAD), axis=1)
                parts.append(jnp.exp2(scores - wide).astype(jnp.bfloat16))
            weights = jnp.concatenate(parts, axis=0)
            extended = jnp.concatenate([get_v(cols), ones], axis=1)
            both = jnp.dot(weights, extended, preferred_element_type=jnp.float32)
            if first:
                mixed[head] = both[:, :HEAD]
                total[head] = both[:, HEAD:]
            else:
                factor = jnp.concatenate(shrink, axis=0)
                new_mixed = mixed[head] * factor + both[:, :HEAD]
                new_total = total[head] * factor + both[:, HEAD:]
                if final:
                    o_ref[:, cols] = (new_mixed / new_total).astype(o_ref.dtype)
                else:
                    mixed[head] = new_mixed
                    total[head] = new_total
            return carry

        low, high = (0, heads) if bounds is None else bounds
        lax.fori_loop(low, high, one_head, 0)

    attend(
        lambda cols: k_own[:, cols],
        lambda cols: v_own[:, cols],
        lambda tile: near_bias[tile : tile + 1, : blocks * BLOCK],
        blocks * BLOCK,
        first=True,
    )

    def halo(side, delta):
        @pl.when(slab_exists(delta))
        def _():
            for copy in halo_copies(side, delta):
                copy.wait_recv()
            start = (blocks + side) * BLOCK
            attend(
                lambda cols: k_halo[side, :, cols],
                lambda cols: v_halo[side, :, cols],
                lambda tile: near_bias[tile : tile + 1, start : start + BLOCK],
                BLOCK,
            )

    halo(0, -1)
    halo(1, 1)

    def band_wait(bit, side, part):
        slot = 2 * bit + side
        for which, (src, dst) in enumerate(((k_hbm, k_band), (v_hbm, v_band))):
            pltpu.make_async_remote_copy(
                src_ref=src.reshape(picks, 2, BLOCK, width).at[:, 0, :, part_cols(part)],
                dst_ref=dst.at[slot, :, :, part_cols(part)],
                send_sem=band_send.at[slot, part, which],
                recv_sem=band_recv.at[slot, part, which],
                device_id={"tm": frame},
                device_id_type=MESH,
            ).wait_recv()

    early = frame < half
    outer = (frame < 2) | (frame >= tm_count - 2)
    corner = (frame == 0) | (frame == tm_count - 1)
    inward = flag(early)
    last = bits - 1
    relay_pair = (
        (outer, lambda part: relay_copies(
            0, 2 + inward, 3 - inward, part, jnp.where(early, frame + half, frame - half))),
        (corner, lambda part: relay_copies(
            1, 2 * last + inward, inward, part, jnp.where(early, half - 1, half))),
    )
    if relayed:
        for part in range(parts):
            for (pred, make), bit in zip(relay_pair, (1, last)):

                @pl.when(pred)
                def _(make=make, bit=bit, part=part):
                    band_wait(bit, inward, part)
                    for copy in make(part):
                        copy.start()

    def band_exists(bit, side):
        return exists(jnp.where(side == 0, -(1 << bit), 1 << bit))

    def band_keys(slot):
        return (
            lambda cols: k_band[slot, :, :, cols].reshape(picks * BLOCK, HEAD),
            lambda cols: v_band[slot, :, :, cols].reshape(picks * BLOCK, HEAD),
            lambda tile: band_bias[slot, tile : tile + 1, :],
        )

    def band(bit, side, waited):
        @pl.when(band_exists(bit, side))
        def _():
            @pl.when(jnp.logical_not(waited))
            def _():
                for part in range(parts):
                    band_wait(bit, side, part)

            attend(*band_keys(2 * bit + side), picks * BLOCK)

    never = frame < 0
    other = 1 - inward
    core_side = 1 - lax.rem(frame, 2)
    relay_a = corner if relayed else never
    relay_b = outer if relayed else never
    band(0, core_side, never)
    for bit in range(2, bits - 1):
        band(bit, other, never)
        band(bit, inward, never)
    band(last, inward, relay_a)
    band(1, other, never)

    late = ((0, 1 - core_side, never), (1, inward, relay_b))
    both_exist = band_exists(0, 1 - core_side) & band_exists(1, inward)
    heads_part = heads // parts

    @pl.when(both_exist)
    def _():
        getters = [band_keys(2 * bit + side) for bit, side, _ in late]

        def joined(index, axis):
            return lambda arg: jnp.concatenate([g[index](arg) for g in getters], axis=axis)

        def one_part(part, carry):
            for bit, side, waited in late:

                @pl.when(jnp.logical_not(waited))
                def _(bit=bit, side=side):
                    band_wait(bit, side, part)

            attend(
                joined(0, 0), joined(1, 0), joined(2, 1), 2 * picks * BLOCK,
                final=True, bounds=(part * heads_part, (part + 1) * heads_part),
            )
            return carry

        lax.fori_loop(0, parts, one_part, 0)

    @pl.when(jnp.logical_not(both_exist))
    def _():
        for bit, side, waited in late:
            band(bit, side, waited)

        def finish(head, carry):
            cols = pl.ds(pl.multiple_of(head * HEAD, HEAD), HEAD)
            o_ref[:, cols] = (mixed[head] / total[head]).astype(o_ref.dtype)
            return carry

        lax.fori_loop(0, heads, finish, 0)

    for side, delta in ((0, 1), (1, -1)):

        @pl.when(slab_exists(delta))
        def _(side=side, delta=delta):
            for copy in halo_copies(side, delta):
                copy.wait_send()

    for bit in range(bits):
        for side in (0, 1):
            pred, device = sends(bit, side)

            @pl.when(pred)
            def _(bit=bit, side=side, device=device):
                for part in range(parts):
                    for copy in band_copies(bit, side, part, device):
                        copy.wait_send()

    if relayed:
        for pred, make in relay_pair:

            @pl.when(pred)
            def _(make=make):
                for part in range(parts):
                    for copy in make(part):
                        copy.wait_send()


def shards(tm_count, space_count, queries, key_rows, value_rows, block_list, block_count):
    rows, width = queries.shape
    blocks = rows // BLOCK
    picks = blocks // 2
    heads = width // HEAD
    slots = 2 * (tm_count.bit_length() - 1)
    kind = key_rows.dtype
    parts = math.gcd(heads, 6)
    in_hbm = pl.BlockSpec(memory_space=pltpu.HBM)
    dma = pltpu.SemaphoreType.DMA
    return pl.pallas_call(
        functools.partial(kernel, tm_count, space_count, block_list.shape[1], parts),
        out_shape=jax.ShapeDtypeStruct((rows, width), queries.dtype),
        in_specs=[in_hbm] * 5,
        out_specs=pl.BlockSpec(memory_space=pltpu.VMEM),
        scratch_shapes=[
            pltpu.SMEM(block_list.shape, block_list.dtype),
            pltpu.SMEM(block_count.shape, block_count.dtype),
            pltpu.VMEM((rows, width), kind),
            pltpu.VMEM((rows, width), kind),
            pltpu.VMEM((rows, width), kind),
            pltpu.VMEM((2, BLOCK, width), kind),
            pltpu.VMEM((2, BLOCK, width), kind),
            pltpu.VMEM((slots, picks, BLOCK, width), kind),
            pltpu.VMEM((slots, picks, BLOCK, width), kind),
            pltpu.VMEM((heads, rows, HEAD), jnp.float32),
            pltpu.VMEM((heads, rows, HEAD), jnp.float32),
            pltpu.VMEM((heads, rows, HEAD), jnp.float32),
            pltpu.VMEM((blocks, (blocks + 2) * BLOCK), jnp.float32),
            pltpu.VMEM((slots, blocks, picks * BLOCK), jnp.float32),
            dma((5,)),
            dma((2, 2)),
            dma((2, 2)),
            dma((slots, parts, 2)),
            dma((slots, parts, 2)),
            dma((2, parts, 2)),
        ],
        compiler_params=pltpu.CompilerParams(
            collective_id=0, has_side_effects=True, vmem_limit_bytes=44 * 1024 * 1024
        ),
    )(*[
        pltpu.with_memory_space_constraint(array, pltpu.HBM)
        for array in (queries, key_rows, value_rows, block_list, block_count)
    ])


def solution(mesh):
    placed = (
        P(("tm", "space"), None),
        P(("tm", "space"), None),
        P(("tm", "space"), None),
        P(("tm", "space"), None),
        P(("tm", "space")),
    )
    return jax.shard_map(
        functools.partial(shards, mesh.shape["tm"], mesh.shape["space"]),
        mesh=mesh, in_specs=placed, out_specs=P(("tm", "space"), None), check_vma=False,
    )
```

```python
import functools
import math

import jax
import jax.numpy as jnp
from jax import lax
from jax.experimental import pallas as pl
from jax.experimental.pallas import tpu as pltpu
from jax.sharding import PartitionSpec as P

HEAD = 128
BLOCK = 128
DEAD = -1e30
MESH = pl.DeviceIdType.MESH


def head_spans(heads):
    spans, start = [], 0
    while start < heads:
        count = max(1, (heads - start) // 2)
        spans.append((start, count))
        start += count
    return spans


def kernel(
    tm_count, space_count, list_width,
    q_hbm, k_hbm, v_hbm, list_hbm, count_hbm, o_ref,
    list_ref, count_ref,
    q_own, k_own, v_own, k_halo, v_halo, k_band, v_band,
    top, total, mixed, near_bias, band_bias,
    local_sem, halo_send, halo_recv, band_send, band_recv, relay_send,
):
    rows, width = q_hbm.shape
    blocks = rows // BLOCK
    picks = blocks // 2
    heads = width // HEAD
    bits = tm_count.bit_length() - 1
    half = tm_count // 2
    relayed = bits == 3
    frame = lax.axis_index("tm")
    slab = lax.axis_index("space")
    scale = math.log2(math.e) / HEAD**0.5

    def flag(pred):
        return jnp.where(pred, 1, 0)

    def exists(delta):
        return (frame + delta >= 0) & (frame + delta < tm_count)

    def slab_exists(delta):
        return (slab + delta >= 0) & (slab + delta < space_count)

    def sends(bit, side):
        delta = (1 << bit) if side == 0 else -(1 << bit)
        pred = exists(delta)
        if relayed and bit == 0:
            pred = pred & (frame != (half - 1 if side == 0 else half))
        if relayed and bit == 1:
            if side == 0:
                pred = pred & ((frame < half - 2) | (frame >= half))
            else:
                pred = pred & ((frame < half) | (frame >= half + 2))
        return pred, frame + delta

    barrier = pltpu.get_barrier_semaphore()
    greets = []
    for delta in (-1, 1):
        greets.append((slab_exists(delta), {"space": slab + delta}))
    for bit in range(bits):
        for side in (0, 1):
            pred, device = sends(bit, side)
            greets.append((pred, {"tm": device}))
    if relayed:
        greets.append((frame == 0, {"tm": frame + half - 1}))
        greets.append((frame == half - 1, {"tm": frame - half + 1}))
        greets.append((frame == tm_count - 1, {"tm": frame - half + 1}))
        greets.append((frame == half, {"tm": frame + half - 1}))
    expected = 0
    for pred, device in greets:
        expected = expected + flag(pred)

        @pl.when(pred)
        def _(device=device):
            pl.semaphore_signal(barrier, inc=1, device_id=device, device_id_type=MESH)

    pl.semaphore_wait(barrier, expected)

    def halo_copies(side, delta):
        start = (blocks - 1) * BLOCK if side == 0 else 0
        for index, (src, dst) in enumerate(((k_hbm, k_halo), (v_hbm, v_halo))):
            yield pltpu.make_async_remote_copy(
                src_ref=src.at[pl.ds(start, BLOCK)],
                dst_ref=dst.at[side],
                send_sem=halo_send.at[side, index],
                recv_sem=halo_recv.at[side, index],
                device_id={"space": slab + delta},
                device_id_type=MESH,
            )

    spans = head_spans(heads)
    parts = len(spans)

    def part_cols(part):
        start, count = spans[part]
        return pl.ds(start * HEAD, count * HEAD)

    def band_copies(bit, side, part, device):
        slot = 2 * bit + side
        for which, (src, dst) in enumerate(((k_hbm, k_band), (v_hbm, v_band))):
            yield pltpu.make_async_remote_copy(
                src_ref=src.reshape(picks, 2, BLOCK, width).at[:, bit % 2, :, part_cols(part)],
                dst_ref=dst.at[slot, :, :, part_cols(part)],
                send_sem=band_send.at[slot, part, which],
                recv_sem=band_recv.at[slot, part, which],
                device_id={"tm": device},
                device_id_type=MESH,
            )

    def relay_copies(kind, slot_from, slot_to, part, device):
        for which, buf in enumerate((k_band, v_band)):
            yield pltpu.make_async_remote_copy(
                src_ref=buf.at[slot_from, :, :, part_cols(part)],
                dst_ref=buf.at[slot_to, :, :, part_cols(part)],
                send_sem=relay_send.at[kind, part, which],
                recv_sem=band_recv.at[slot_to, part, which],
                device_id={"tm": device},
                device_id_type=MESH,
            )

    for side, delta in ((0, 1), (1, -1)):

        @pl.when(slab_exists(delta))
        def _(side=side, delta=delta):
            for copy in halo_copies(side, delta):
                copy.start()

    order = list(range(1, bits)) + [0]
    for bit in order:
        for side in (0, 1):
            pred, device = sends(bit, side)

            @pl.when(pred)
            def _(bit=bit, side=side, device=device):
                for part in range(parts):
                    for copy in band_copies(bit, side, part, device):
                        copy.start()

    local = [
        pltpu.make_async_copy(src, dst, local_sem.at[index])
        for index, (src, dst) in enumerate((
            (q_hbm, q_own), (k_hbm, k_own), (v_hbm, v_own),
            (list_hbm, list_ref), (count_hbm, count_ref),
        ))
    ]
    for copy in local:
        copy.start()

    for copy in local[3:]:
        copy.wait()

    frame_blocks = blocks * space_count
    first_block = frame * frame_blocks + slab * blocks

    def bias_rows(ids):
        row = jnp.concatenate([jnp.full((1, BLOCK), ident, jnp.int32) for ident in ids], axis=1)
        out = []
        for tile in range(blocks):
            count = count_ref[tile]
            value = jnp.full(row.shape, DEAD, jnp.float32)
            for entry in range(list_width):
                listed = jnp.where(entry < count, list_ref[tile, entry], -1)
                value = jnp.where(row == listed, 0.0, value)
            out.append(value)
        return out

    near_ids = [first_block + c for c in range(blocks)] + [first_block - 1, first_block + blocks]
    for tile, value in enumerate(bias_rows(near_ids)):
        near_bias[tile : tile + 1, :] = value
    for bit in range(bits):
        for side in (0, 1):
            partner = frame - (1 << bit) if side == 0 else frame + (1 << bit)
            ids = [
                partner * frame_blocks + slab * blocks + 2 * pick + bit % 2
                for pick in range(picks)
            ]
            for tile, value in enumerate(bias_rows(ids)):
                band_bias[2 * bit + side, tile : tile + 1, :] = value

    for copy in local[:3]:
        copy.wait()

    def attend(get_k, get_v, get_bias, keys, first=False, final=False, bounds=None):
        ones = jnp.ones((keys, HEAD), jnp.bfloat16)

        def one_head(head, carry):
            cols = pl.ds(pl.multiple_of(head * HEAD, HEAD), HEAD)
            raw = lax.dot_general(
                q_own[:, cols], get_k(cols), (((1,), (1,)), ((), ())),
                preferred_element_type=jnp.float32,
            )
            parts, shrink = [], []
            for tile in range(blocks):
                span = slice(tile * BLOCK, (tile + 1) * BLOCK)
                scores = raw[span] * scale + get_bias(tile)
                peak = jnp.max(scores, axis=1, keepdims=True)
                if first:
                    new_top = jnp.broadcast_to(peak, (BLOCK, HEAD))
                else:
                    old_top = top[head, span, :]
                    new_top = jnp.maximum(old_top, peak)
                    shrink.append(jnp.exp2(old_top - new_top))
                if not final:
                    top[head, span, :] = new_top
                wide = jnp.concatenate([new_top] * (keys // HEAD), axis=1)
                parts.append(jnp.exp2(scores - wide).astype(jnp.bfloat16))
            weights = jnp.concatenate(parts, axis=0)
            extended = jnp.concatenate([get_v(cols), ones], axis=1)
            both = jnp.dot(weights, extended, preferred_element_type=jnp.float32)
            if first:
                mixed[head] = both[:, :HEAD]
                total[head] = both[:, HEAD:]
            else:
                factor = jnp.concatenate(shrink, axis=0)
                new_mixed = mixed[head] * factor + both[:, :HEAD]
                new_total = total[head] * factor + both[:, HEAD:]
                if final:
                    o_ref[:, cols] = (new_mixed / new_total).astype(o_ref.dtype)
                else:
                    mixed[head] = new_mixed
                    total[head] = new_total
            return carry

        start, count = (0, heads) if bounds is None else bounds
        paired = count - count % 2
        if paired > 2:
            lax.fori_loop(start, start + paired, one_head, 0, unroll=2)
        for head in range(start if paired <= 2 else start + paired, start + count):
            one_head(head, 0)

    attend(
        lambda cols: k_own[:, cols],
        lambda cols: v_own[:, cols],
        lambda tile: near_bias[tile : tile + 1, : blocks * BLOCK],
        blocks * BLOCK,
        first=True,
    )

    def halo(side, delta):
        @pl.when(slab_exists(delta))
        def _():
            for copy in halo_copies(side, delta):
                copy.wait_recv()
            start = (blocks + side) * BLOCK
            attend(
                lambda cols: k_halo[side, :, cols],
                lambda cols: v_halo[side, :, cols],
                lambda tile: near_bias[tile : tile + 1, start : start + BLOCK],
                BLOCK,
            )

    halo(0, -1)
    halo(1, 1)

    def band_wait(bit, side, part):
        slot = 2 * bit + side
        for which, (src, dst) in enumerate(((k_hbm, k_band), (v_hbm, v_band))):
            pltpu.make_async_remote_copy(
                src_ref=src.reshape(picks, 2, BLOCK, width).at[:, 0, :, part_cols(part)],
                dst_ref=dst.at[slot, :, :, part_cols(part)],
                send_sem=band_send.at[slot, part, which],
                recv_sem=band_recv.at[slot, part, which],
                device_id={"tm": frame},
                device_id_type=MESH,
            ).wait_recv()

    early = frame < half
    outer = (frame < 2) | (frame >= tm_count - 2)
    corner = (frame == 0) | (frame == tm_count - 1)
    inward = flag(early)
    last = bits - 1
    relay_pair = (
        (outer, lambda part: relay_copies(
            0, 2 + inward, 3 - inward, part, jnp.where(early, frame + half, frame - half))),
        (corner, lambda part: relay_copies(
            1, 2 * last + inward, inward, part, jnp.where(early, half - 1, half))),
    )
    if relayed:
        for part in range(parts):
            for (pred, make), bit in zip(relay_pair, (1, last)):

                @pl.when(pred)
                def _(make=make, bit=bit, part=part):
                    band_wait(bit, inward, part)
                    for copy in make(part):
                        copy.start()

    def band_exists(bit, side):
        return exists(jnp.where(side == 0, -(1 << bit), 1 << bit))

    def band_keys(slot):
        return (
            lambda cols: k_band[slot, :, :, cols].reshape(picks * BLOCK, HEAD),
            lambda cols: v_band[slot, :, :, cols].reshape(picks * BLOCK, HEAD),
            lambda tile: band_bias[slot, tile : tile + 1, :],
        )

    def band(bit, side, waited):
        @pl.when(band_exists(bit, side))
        def _():
            @pl.when(jnp.logical_not(waited))
            def _():
                for part in range(parts):
                    band_wait(bit, side, part)

            attend(*band_keys(2 * bit + side), picks * BLOCK)

    never = frame < 0
    other = 1 - inward
    core_side = 1 - lax.rem(frame, 2)
    relay_a = corner if relayed else never
    relay_b = outer if relayed else never
    band(0, core_side, never)
    for bit in range(2, bits - 1):
        band(bit, other, never)
        band(bit, inward, never)
    band(last, inward, relay_a)
    band(1, other, never)

    late = ((0, 1 - core_side, never), (1, inward, relay_b))
    both_exist = band_exists(0, 1 - core_side) & band_exists(1, inward)
    heads_part = heads // parts

    @pl.when(both_exist)
    def _():
        getters = [band_keys(2 * bit + side) for bit, side, _ in late]

        def joined(index, axis):
            return lambda arg: jnp.concatenate([g[index](arg) for g in getters], axis=axis)

        for part in range(parts):
            for bit, side, waited in late:

                @pl.when(jnp.logical_not(waited))
                def _(bit=bit, side=side, part=part):
                    band_wait(bit, side, part)

            attend(
                joined(0, 0), joined(1, 0), joined(2, 1), 2 * picks * BLOCK,
                final=True, bounds=spans[part],
            )

    @pl.when(jnp.logical_not(both_exist))
    def _():
        for bit, side, waited in late:
            band(bit, side, waited)

        def finish(head, carry):
            cols = pl.ds(pl.multiple_of(head * HEAD, HEAD), HEAD)
            o_ref[:, cols] = (mixed[head] / total[head]).astype(o_ref.dtype)
            return carry

        lax.fori_loop(0, heads, finish, 0)

    for side, delta in ((0, 1), (1, -1)):

        @pl.when(slab_exists(delta))
        def _(side=side, delta=delta):
            for copy in halo_copies(side, delta):
                copy.wait_send()

    for bit in range(bits):
        for side in (0, 1):
            pred, device = sends(bit, side)

            @pl.when(pred)
            def _(bit=bit, side=side, device=device):
                for part in range(parts):
                    for copy in band_copies(bit, side, part, device):
                        copy.wait_send()

    if relayed:
        for pred, make in relay_pair:

            @pl.when(pred)
            def _(make=make):
                for part in range(parts):
                    for copy in make(part):
                        copy.wait_send()


def shards(tm_count, space_count, queries, key_rows, value_rows, block_list, block_count):
    rows, width = queries.shape
    blocks = rows // BLOCK
    picks = blocks // 2
    heads = width // HEAD
    slots = 2 * (tm_count.bit_length() - 1)
    kind = key_rows.dtype
    parts = len(head_spans(heads))
    in_hbm = pl.BlockSpec(memory_space=pltpu.HBM)
    dma = pltpu.SemaphoreType.DMA
    return pl.pallas_call(
        functools.partial(kernel, tm_count, space_count, block_list.shape[1]),
        out_shape=jax.ShapeDtypeStruct((rows, width), queries.dtype),
        in_specs=[in_hbm] * 5,
        out_specs=pl.BlockSpec(memory_space=pltpu.VMEM),
        scratch_shapes=[
            pltpu.SMEM(block_list.shape, block_list.dtype),
            pltpu.SMEM(block_count.shape, block_count.dtype),
            pltpu.VMEM((rows, width), kind),
            pltpu.VMEM((rows, width), kind),
            pltpu.VMEM((rows, width), kind),
            pltpu.VMEM((2, BLOCK, width), kind),
            pltpu.VMEM((2, BLOCK, width), kind),
            pltpu.VMEM((slots, picks, BLOCK, width), kind),
            pltpu.VMEM((slots, picks, BLOCK, width), kind),
            pltpu.VMEM((heads, rows, HEAD), jnp.float32),
            pltpu.VMEM((heads, rows, HEAD), jnp.float32),
            pltpu.VMEM((heads, rows, HEAD), jnp.float32),
            pltpu.VMEM((blocks, (blocks + 2) * BLOCK), jnp.float32),
            pltpu.VMEM((slots, blocks, picks * BLOCK), jnp.float32),
            dma((5,)),
            dma((2, 2)),
            dma((2, 2)),
            dma((slots, parts, 2)),
            dma((slots, parts, 2)),
            dma((2, parts, 2)),
        ],
        compiler_params=pltpu.CompilerParams(
            collective_id=0, has_side_effects=True, vmem_limit_bytes=44 * 1024 * 1024
        ),
    )(*[
        pltpu.with_memory_space_constraint(array, pltpu.HBM)
        for array in (queries, key_rows, value_rows, block_list, block_count)
    ])


def solution(mesh):
    placed = (
        P(("tm", "space"), None),
        P(("tm", "space"), None),
        P(("tm", "space"), None),
        P(("tm", "space"), None),
        P(("tm", "space")),
    )
    return jax.shard_map(
        functools.partial(shards, mesh.shape["tm"], mesh.shape["space"]),
        mesh=mesh, in_specs=placed, out_specs=P(("tm", "space"), None), check_vma=False,
    )
```
